32 devices in a mesh: seq: 4 (over x, core), expert: 8 (over z, y).
Axes of the slice: x: 2, y: 2, z: 4, core: 2. Of those that a mesh axis runs over, the one named last changes fastest.
Arguments:
- hidden_in: bfloat16 [4096, 2048], P(('seq', 'expert')), may hold values from -6 to 6
- d_output: bfloat16 [4096, 2048], P(('seq', 'expert')), may hold values from -6 to 6
- gain: float32 [2048], replicated, may hold values from 0.5 to 1.5
- route_ids: int32 [4096, 4], P(('seq', 'expert')), may hold values from 0 to 31, all different within a row; in each aligned block of 128 rows (0 to 127, 128 to 255, ...) at most 24 rows name the same one
- gates: bfloat16 [4096, 4], P(('seq', 'expert')), may hold values from 0.049804688 to 0.59765625
- w_gate: bfloat16 [32, 2048, 768], P(('seq', 'expert')), may hold values from -0.125 to 0.125
- w_up: bfloat16 [32, 2048, 768], P(('seq', 'expert')), may hold values from -0.125 to 0.125
- w_down: bfloat16 [32, 768, 2048], P(('seq', 'expert')), may hold values from -0.21875 to 0.21875
Outputs:
- d_hidden_in: bfloat16 [4096, 2048], P(('seq', 'expert'))
- d_gain: float32 [2048], P(('seq', 'expert'))
- d_gates: bfloat16 [4096, 4], P(('seq', 'expert'))
- d_w_gate: bfloat16 [32, 2048, 768], P(('seq', 'expert'))
- d_w_up: bfloat16 [32, 2048, 768], P(('seq', 'expert'))
- d_w_down: bfloat16 [32, 768, 2048], P(('seq', 'expert'))
The draws below stay inside these ranges and needn't reach their ends.
Inputs may be any that keep to these rules, and one draw needn't show every extreme that they name: `route_ids`: each row names 4 different experts. Within the 128 rows of one device no expert is named by more than 24 rows, and in every draw some expert is named by exactly 24 rows of some device.
All inputs are finite; a program needn't handle non-finite values.
Results may differ from the reference program's by a relative error of at most 0.0073.
Values may be sent and summed in bfloat16 or wider, within the bound.
A program may use at most 128 MiB of HBM per device.

```python
import math
import jax
import jax.numpy as jnp
import numpy as np
from jax import lax

D = 2048
FF = 768
TOP = 4
TOK_DEV = 128
EXPERTS = 32
TOKENS = 4096
CAP = 24
DEVICES = 32


def strengthened(array, key, source, target, parts, factor):
    owner, partner = [(jnp.arange(array.shape[dim]) // (array.shape[dim] // parts)).reshape([-1 if axis == dim else 1 for axis in range(array.ndim)]) for dim in (source, target)]
    chosen = jax.random.permutation(key, parts)[partner]
    strong = (owner == chosen) | (owner == (partner + parts // 2) % parts)
    return jnp.where(strong, factor * array, array)


def shard_levels(rng, dims, split, least, largest):
    def one(dim, blocks):
        heights = jax.random.uniform(jax.random.fold_in(jax.random.fold_in(rng, 6), dim), (blocks,), jnp.float32, least / len(split), largest / len(split))
        return jnp.repeat(jnp.exp(heights), dims[dim] // blocks).reshape((-1,) + (1,) * (len(dims) - dim - 1))

    loudness = one(*split[0])
    for cut in split[1:]:
        loudness = loudness * one(*cut)
    return loudness


def deal_out(stream_key, own, number, rows, amount, top, reach, lean):
    ranking = jax.random.permutation(stream_key, amount)
    heavy_load, common = portions_of(amount, rows * top, reach, lean, True), portions_of(amount, rows * top, reach, lean, False)
    places = jnp.arange(amount)

    def named(sizes, rotation):
        used = int((sizes > 0).sum())
        fixed = max(1, used // 4)
        passed = fixed + (places - fixed + rotation * (used - fixed)) % max(1, amount - fixed)
        return jnp.zeros((amount,), jnp.int32).at[ranking[jnp.where(places < fixed, places, passed)]].set(jnp.asarray(sizes, jnp.int32))

    sizes = jnp.where(number % 4 == 0, named(heavy_load, number // 4), named(common, number - number // 4 - 1))
    mixed = jax.random.permutation(jax.random.fold_in(own, 3), amount)
    giver, sink = mixed[0:amount // 2 * 2:2], mixed[1:amount // 2 * 2:2]
    room = jnp.minimum(sizes[giver] - 1, reach - sizes[sink]) // 2
    room = jnp.where((giver == ranking[0]) | (sink == ranking[0]) | (sizes[sink] == 0), 0, jnp.maximum(room, 0))
    passed = jax.random.randint(jax.random.fold_in(own, 4), (amount // 2,), 0, 1 << 20) % (room + 1)
    sizes = sizes.at[giver].add(-passed).at[sink].add(passed)
    items = jnp.searchsorted(jnp.cumsum(sizes), jnp.arange(rows * top), side="right").astype(jnp.int32)
    listing = items.reshape(top, rows).T
    listing = listing[jax.random.permutation(jax.random.fold_in(own, 1), rows)]
    rotation = jax.random.randint(jax.random.fold_in(own, 2), (rows, 1), 0, top)
    return jnp.take_along_axis(listing, (jnp.arange(top)[None, :] + rotation) % top, axis=1)


def portions_of(count, total, most, skew, full):
    weights = [(1 << 20) // math.isqrt(grade ** skew) + 1 for grade in range(1, count + 1)]
    largest = most if full else min(most, max(-(-total // count), total * weights[0] // sum(weights)))
    least = 1 if total - largest >= count - 1 else 0
    holding, rest = [largest] + [least] * (count - 1), total - largest - least * (count - 1)
    while rest > 0:
        movable = [i for i in range(1, count) if holding[i] < largest] or [i for i in range(1, count) if holding[i] < most]
        mass, budget = sum([weights[i] for i in movable]), rest
        for i in movable:
            extra = min(most - holding[i], max(1, budget * weights[i] // mass), rest)
            holding[i] = holding[i] + extra
            rest = rest - extra
    return np.array(holding)


def noise(stream_key, shape, scale, limit, cuts=(), kind=jnp.bfloat16):
    level = shard_levels(stream_key, shape, cuts, -0.22, 0.18) if cuts else 1.0
    values = jax.random.normal(stream_key, shape, jnp.float32) * scale * level
    return jnp.minimum(jnp.maximum(values, -limit), limit).astype(kind)


def heavy_noise(own_key, extent, width, most, shards, heavy, kind=jnp.bfloat16):
    result = width * jax.random.normal(own_key, extent, jnp.float32)
    if shards:
        result = result * shard_levels(own_key, extent, shards, -0.22, 0.18)
    return jnp.clip(strengthened(result, jax.random.fold_in(own_key, 3), *heavy), -most, most).astype(kind)


def setup_inputs(seed: int = 0) -> dict:
    seeds = jax.random.split(jax.random.key(seed), 9)
    hidden_in = heavy_noise(seeds[0], (TOKENS, D), 1.0, 6.0, ((0, 32),), (0, 1, 32, 2.75))
    d_output = noise(seeds[1], (TOKENS, D), 1.0, 6.0, ((0, 32),))
    gain = jnp.clip(1.0 + 0.1 * jax.random.normal(seeds[2], (D,), jnp.float32), 0.5, 1.5)
    route_ids_keys = jax.random.split(jax.random.fold_in(seeds[3], 1), TOKENS // TOK_DEV)
    route_ids_turns = jax.random.permutation(jax.random.fold_in(seeds[3], 3), TOKENS // TOK_DEV)
    route_ids = jax.vmap(lambda own, number: deal_out(jax.random.fold_in(seeds[3], 2), own, number, TOK_DEV, EXPERTS, TOP, CAP, 2))(route_ids_keys, route_ids_turns).reshape((TOKENS, TOP))
    gates = jnp.clip(0.049804688 + 0.54785156 * jax.random.uniform(seeds[4], (TOKENS, TOP), jnp.float32) ** shard_levels(seeds[4], (TOKENS, TOP), ((0, 32),), -0.2, 0.2), 0.049804688, 0.59765625).astype(jnp.bfloat16)
    w_gate = noise(seeds[5], (EXPERTS, D, FF), D ** -0.5, 0.125, ((0, 32),))
    w_up = noise(seeds[6], (EXPERTS, D, FF), D ** -0.5, 0.125, ((0, 32),))
    w_down = noise(seeds[7], (EXPERTS, FF, D), FF ** -0.5, 0.21875, ((0, 32),))
    return {"hidden_in": hidden_in, "d_output": d_output, "gain": gain, "route_ids": route_ids, "gates": gates, "w_gate": w_gate, "w_up": w_up, "w_down": w_down}


def slot_index(block_ids):
    flat_ids = block_ids.reshape(-1)
    onehot = (flat_ids[:, None] == jnp.arange(EXPERTS, dtype=jnp.int32)[None, :]).astype(jnp.int32)
    before = jnp.cumsum(onehot, axis=0) - onehot
    position = lax.optimization_barrier(jnp.sum(before * onehot, axis=1)).astype(jnp.int32)
    return (flat_ids * CAP + position).astype(jnp.int32)

def expert_backward(operands):
    rows_in, rows_cot, rows_gate, gate_w, up_w, down_w = operands
    pre_gate = jnp.dot(rows_in, gate_w, preferred_element_type=jnp.float32)
    pre_up = jnp.dot(rows_in, up_w, preferred_element_type=jnp.float32)
    sigmoid_gate = jax.nn.sigmoid(pre_gate)
    silu_gate = pre_gate * sigmoid_gate
    act = (silu_gate * pre_up).astype(jnp.bfloat16)
    expert_out = jnp.dot(act, down_w, preferred_element_type=jnp.float32)
    slot_grad = lax.optimization_barrier(jnp.sum(rows_cot.astype(jnp.float32) * expert_out, axis=1)).astype(jnp.bfloat16)
    d_expert = (rows_gate.astype(jnp.float32)[:, None] * rows_cot.astype(jnp.float32)).astype(jnp.bfloat16)
    d_act = jnp.dot(d_expert, down_w.T, preferred_element_type=jnp.float32)
    grad_gate = (d_act * pre_up * sigmoid_gate * (1.0 + pre_gate * (1.0 - sigmoid_gate))).astype(jnp.bfloat16)
    grad_up = (d_act * silu_gate).astype(jnp.bfloat16)
    grad_down_w = jnp.dot(act.T, d_expert, preferred_element_type=jnp.float32).astype(jnp.bfloat16)
    grad_gate_w = jnp.dot(rows_in.T, grad_gate, preferred_element_type=jnp.float32).astype(jnp.bfloat16)
    grad_up_w = jnp.dot(rows_in.T, grad_up, preferred_element_type=jnp.float32).astype(jnp.bfloat16)
    d_rows = (jnp.dot(grad_gate, gate_w.T, preferred_element_type=jnp.float32) + jnp.dot(grad_up, up_w.T, preferred_element_type=jnp.float32)).astype(jnp.bfloat16)
    return (d_rows, slot_grad, grad_gate_w, grad_up_w, grad_down_w)

def reference(hidden_in, d_output, gain, route_ids, gates, w_gate, w_up, w_down):
    wide_rows = hidden_in.astype(jnp.float32)
    inverse_rms = lax.rsqrt(lax.optimization_barrier(jnp.mean(wide_rows * wide_rows, axis=1, keepdims=True)) + 1e-06)
    unit_rows = wide_rows * inverse_rms
    normed = (unit_rows * gain[None, :]).astype(jnp.bfloat16)
    slots = jax.vmap(slot_index)(route_ids.reshape(DEVICES, TOK_DEV, TOP))
    pair_in = jnp.broadcast_to(normed.reshape(DEVICES, TOK_DEV, 1, D), (DEVICES, TOK_DEV, TOP, D)).reshape(DEVICES, TOK_DEV * TOP, D)
    pair_cot = jnp.broadcast_to(d_output.reshape(DEVICES, TOK_DEV, 1, D), (DEVICES, TOK_DEV, TOP, D)).reshape(DEVICES, TOK_DEV * TOP, D)
    pair_gate = gates.reshape(DEVICES, TOK_DEV * TOP)

    def place_rows(slot_list, values):
        empty = jnp.zeros((EXPERTS * CAP,) + values.shape[1:], values.dtype)
        return empty.at[slot_list].set(values)
    buf_in = jax.vmap(place_rows)(slots, pair_in)
    buf_cot = jax.vmap(place_rows)(slots, pair_cot)
    buf_gate = jax.vmap(place_rows)(slots, pair_gate)
    by_expert_in = buf_in.reshape(DEVICES, EXPERTS, CAP, D).transpose(1, 0, 2, 3).reshape(EXPERTS, DEVICES * CAP, D)
    by_expert_cot = buf_cot.reshape(DEVICES, EXPERTS, CAP, D).transpose(1, 0, 2, 3).reshape(EXPERTS, DEVICES * CAP, D)
    by_expert_gate = buf_gate.reshape(DEVICES, EXPERTS, CAP).transpose(1, 0, 2).reshape(EXPERTS, DEVICES * CAP)
    d_rows, slot_grad, d_w_gate, d_w_up, d_w_down = lax.map(expert_backward, (by_expert_in, by_expert_cot, by_expert_gate, w_gate, w_up, w_down))
    back_rows = d_rows.reshape(EXPERTS, DEVICES, CAP, D).transpose(1, 0, 2, 3).reshape(DEVICES, EXPERTS * CAP, D)
    back_grad = slot_grad.reshape(EXPERTS, DEVICES, CAP).transpose(1, 0, 2).reshape(DEVICES, EXPERTS * CAP)
    pair_rows = jax.vmap(lambda values, slot_list: values[slot_list])(back_rows, slots)
    d_normed = lax.optimization_barrier(jnp.sum(pair_rows.reshape(TOKENS, TOP, D).astype(jnp.float32), axis=1))
    d_gates = jax.vmap(lambda values, slot_list: values[slot_list])(back_grad, slots).reshape(TOKENS, TOP)
    d_gain = lax.optimization_barrier(jnp.sum(d_normed * unit_rows, axis=0))
    d_unit = d_normed * gain[None, :]
    inner = lax.optimization_barrier(jnp.mean(d_unit * unit_rows, axis=1, keepdims=True))
    d_hidden_in = (d_output.astype(jnp.float32) + inverse_rms * (d_unit - unit_rows * inner)).astype(jnp.bfloat16)
    return (d_hidden_in, d_gain, d_gates, d_w_gate, d_w_up, d_w_down)
```

```python
import functools

import jax
import jax.numpy as jnp
from jax import lax
from jax.experimental import pallas as pl
from jax.experimental.pallas import tpu as pltpu
from jax.sharding import PartitionSpec as P

BF = jnp.bfloat16
F32 = jnp.float32
AXES = ("seq", "expert")


def coords(outer, inner):
    s = lax.axis_index("seq")
    e = lax.axis_index("expert")
    return s, e // inner, e % inner


def dispatch_kernel(
    seqs, outer, inner, normed, cot, table, got_in, got_cot, table_all,
    line, table_line, stage, line_send, line_recv, table_send, table_recv,
    plane_send, plane_recv, own_sem,
):
    s, o, i = coords(outer, inner)
    plane = seqs * inner
    p = s * inner + i
    width = normed.shape[1]
    cap = got_in.shape[1]
    barrier = pltpu.get_barrier_semaphore()

    def line_peer(d):
        return (s, ((o + d) % outer) * inner + i)

    def plane_peer(t):
        return (t // inner, o * inner + t % inner)

    for d in range(1, outer):
        pl.semaphore_signal(barrier, inc=1, device_id=line_peer(d), device_id_type=pl.DeviceIdType.MESH)

    def greet(q, carry):
        pl.semaphore_signal(
            barrier, inc=1, device_id=plane_peer((p + q) % plane), device_id_type=pl.DeviceIdType.MESH
        )
        return carry

    lax.fori_loop(1, plane, greet, 0)
    pl.semaphore_wait(barrier, outer - 1 + plane - 1)

    def remote(src, dst, send, recv, peer):
        return pltpu.make_async_remote_copy(
            src_ref=src, dst_ref=dst, send_sem=send, recv_sem=recv,
            device_id=peer, device_id_type=pl.DeviceIdType.MESH,
        )

    sources = (cot, normed)
    targets = (got_cot, got_in)

    def table_copy(d):
        return remote(
            table.at[(o + d) % outer], table_line.at[d], table_send.at[d], table_recv.at[d], line_peer(d)
        )

    def line_copy(t, d):
        return remote(sources[t], line.at[t, d], line_send.at[t, d], line_recv.at[t, d], line_peer(d))

    def plane_copy(t, d, q):
        to = (p + q) % plane
        home = s * (outer * inner) + ((o - d + outer) % outer) * inner + i
        return remote(
            stage.at[t, d, to], targets[t].at[home],
            plane_send.at[t, d, q], plane_recv.at[t, d, q], plane_peer(to),
        )

    def own_copy(t, d):
        home = s * (outer * inner) + ((o - d + outer) % outer) * inner + i
        return pltpu.make_async_copy(stage.at[t, d, p], targets[t].at[home], own_sem.at[t, d])

    def table_out(d):
        src = table.at[o] if d == 0 else table_line.at[d]
        return pltpu.make_async_copy(src, table_all.at[d], table_send.at[d] if d == 0 else table_recv.at[d])

    for d in range(1, outer):
        table_copy(d).start()
    for d in range(1, outer):
        for t in range(2):
            line_copy(t, d).start()

    for d in range(outer):
        if d > 0:
            table_copy(d).wait_recv()
        for t in range(2):
            if d > 0:
                line_copy(t, d).wait_recv()
            step = 512 if width % 512 == 0 else width

            def place(c, carry, t=t, d=d, step=step):
                cols = pl.ds(pl.multiple_of(c * step, step), step)
                rows = sources[t][:, cols] if d == 0 else line[t, d, :, cols]
                pick = table[o] if d == 0 else table_line[d]
                put = jnp.dot(pick, rows, preferred_element_type=F32).astype(BF)
                stage[t, d, :, :, cols] = put.reshape(plane, cap, step)
                return carry

            lax.fori_loop(0, width // step, place, 0)
            own_copy(t, d).start()

            def push(q, carry, t=t, d=d):
                plane_copy(t, d, q).start()
                return carry

            lax.fori_loop(1, plane, push, 0)
        table_out(d).start()

    for d in range(1, outer):
        table_copy(d).wait_send()
        for t in range(2):
            line_copy(t, d).wait_send()
    for d in range(outer):
        table_out(d).wait()
        for t in range(2):
            own_copy(t, d).wait()

            def finish(q, carry, t=t, d=d):
                plane_copy(t, d, q).wait_recv()
                plane_copy(t, d, q).wait_send()
                return carry

            lax.fori_loop(1, plane, finish, 0)


def dispatch(normed, cot, table, seqs, outer, inner, cap):
    rows, width = normed.shape
    plane = seqs * inner
    count = plane * outer
    vmem = pl.BlockSpec(memory_space=pltpu.VMEM)
    anywhere = pl.BlockSpec(memory_space=pl.ANY)
    dma = pltpu.SemaphoreType.DMA
    return pl.pallas_call(
        functools.partial(dispatch_kernel, seqs, outer, inner),
        out_shape=(
            jax.ShapeDtypeStruct((count, cap, width), BF),
            jax.ShapeDtypeStruct((count, cap, width), BF),
            jax.ShapeDtypeStruct(table.shape, BF),
        ),
        in_specs=[vmem, vmem, vmem],
        out_specs=(anywhere, anywhere, anywhere),
        scratch_shapes=[
            pltpu.VMEM((2, outer, rows, width), BF),
            pltpu.VMEM(table.shape, BF),
            pltpu.VMEM((2, outer, plane, cap, width), BF),
            dma((2, outer)),
            dma((2, outer)),
            dma((outer,)),
            dma((outer,)),
            dma((2, outer, plane)),
            dma((2, outer, plane)),
            dma((2, outer)),
        ],
        compiler_params=pltpu.CompilerParams(
            collective_id=0, has_side_effects=True, vmem_limit_bytes=40 * 1024 * 1024
        ),
        name="dispatch",
    )(normed, cot, table)


def expert_backward(rows_in, rows_cot, rows_gate, gate_w, up_w, down_w):
    pre_gate = jnp.dot(rows_in, gate_w, preferred_element_type=F32)
    pre_up = jnp.dot(rows_in, up_w, preferred_element_type=F32)
    sigmoid_gate = jax.nn.sigmoid(pre_gate)
    silu_gate = pre_gate * sigmoid_gate
    act = (silu_gate * pre_up).astype(BF)
    expert_out = jnp.dot(act, down_w, preferred_element_type=F32)
    slot_grad = jnp.sum(rows_cot.astype(F32) * expert_out, axis=1).astype(BF)
    d_expert = (rows_gate.astype(F32)[:, None] * rows_cot.astype(F32)).astype(BF)
    d_act = lax.dot_general(d_expert, down_w, (((1,), (1,)), ((), ())), preferred_element_type=F32)
    grad_gate = (d_act * pre_up * sigmoid_gate * (1.0 + pre_gate * (1.0 - sigmoid_gate))).astype(BF)
    grad_up = (d_act * silu_gate).astype(BF)
    turned = (((0,), (0,)), ((), ()))
    grad_down_w = lax.dot_general(act, d_expert, turned, preferred_element_type=F32).astype(BF)
    grad_gate_w = lax.dot_general(rows_in, grad_gate, turned, preferred_element_type=F32).astype(BF)
    grad_up_w = lax.dot_general(rows_in, grad_up, turned, preferred_element_type=F32).astype(BF)
    across = (((1,), (1,)), ((), ()))
    d_rows = (
        lax.dot_general(grad_gate, gate_w, across, preferred_element_type=F32)
        + lax.dot_general(grad_up, up_w, across, preferred_element_type=F32)
    ).astype(BF)
    return (d_rows, slot_grad, grad_gate_w, grad_up_w, grad_down_w)


def body(hidden_in, d_output, gain, route_ids, gates, w_gate, w_up, w_down):
    tok_rows, width = hidden_in.shape
    top_count = route_ids.shape[1]
    seqs = lax.axis_size("seq")
    per_seq = lax.axis_size("expert")
    outer = 4 if per_seq % 4 == 0 else 2
    inner = per_seq // outer
    devices = seqs * per_seq
    experts = w_gate.shape[0] * devices
    capacity = max(2, tok_rows * top_count * 3 // (2 * experts))
    cap = -(-capacity // 8) * 8
    wide_rows = hidden_in.astype(F32)
    inverse_rms = lax.rsqrt(jnp.mean(wide_rows * wide_rows, axis=1, keepdims=True) + 1e-06)
    unit_rows = wide_rows * inverse_rms
    normed = (unit_rows * gain[None, :]).astype(BF)

    ids_t = route_ids.T
    gates_t = gates.T
    names = jnp.arange(experts, dtype=jnp.int32)
    hit = ids_t[:, None, :] == names[None, :, None]
    chosen = jnp.any(hit, axis=0)
    gate_map = jnp.sum(jnp.where(hit, gates_t[:, None, :].astype(F32), 0.0), axis=0)
    token = jnp.arange(tok_rows, dtype=jnp.int32)
    earlier = (token[:, None] < token[None, :]).astype(BF)
    position = jnp.dot(chosen.astype(BF), earlier, preferred_element_type=F32).astype(jnp.int32)
    placed = chosen[:, None, :] & (position[:, None, :] == jnp.arange(cap, dtype=jnp.int32)[None, :, None])
    table = placed.astype(BF)
    send_gate = jnp.sum(jnp.where(placed, gate_map[:, None, :], 0.0), axis=2).astype(BF)
    got_gate = lax.all_to_all(send_gate, AXES, split_axis=0, concat_axis=0, tiled=True)
    by_plane = (
        table.reshape(seqs, outer, inner, cap, tok_rows)
        .transpose(1, 0, 2, 3, 4)
        .reshape(outer, seqs * inner * cap, tok_rows)
    )
    got_in, got_cot, _ = dispatch(normed, d_output, by_plane, seqs, outer, inner, cap)
    d_rows, slot_grad, grad_gate_w, grad_up_w, grad_down_w = expert_backward(
        got_in.reshape(-1, width), got_cot.reshape(-1, width), got_gate.reshape(-1),
        w_gate[0], w_up[0], w_down[0],
    )
    home_grad = lax.all_to_all(
        slot_grad.reshape(devices, cap), AXES, split_axis=0, concat_axis=0, tiled=True
    )
    home_rows = lax.all_to_all(
        d_rows.reshape(devices, cap, width), AXES, split_axis=0, concat_axis=0, tiled=True
    )
    d_normed = lax.dot_general(
        table.reshape(-1, tok_rows), home_rows.reshape(-1, width), (((0,), (0,)), ((), ())),
        preferred_element_type=F32,
    )
    grad_map = jnp.sum(jnp.where(placed, home_grad[:, :, None].astype(F32), 0.0), axis=1)
    d_gates = jnp.sum(jnp.where(hit, grad_map[None], 0.0), axis=1).astype(BF).T
    gain_term = jnp.sum(d_normed * unit_rows, axis=0)
    gain_parts = lax.all_to_all(
        gain_term.reshape(devices, -1), AXES, split_axis=0, concat_axis=0, tiled=True
    )
    d_gain = jnp.sum(gain_parts, axis=0)
    d_unit = d_normed * gain[None, :]
    inner_mean = jnp.mean(d_unit * unit_rows, axis=1, keepdims=True)
    d_hidden_in = (
        d_output.astype(F32) + inverse_rms * (d_unit - unit_rows * inner_mean)
    ).astype(BF)
    return (d_hidden_in, d_gain, d_gates, grad_gate_w[None], grad_up_w[None], grad_down_w[None])


def solution(mesh):
    rows = P(AXES, None)
    blocks = P(AXES, None, None)
    return jax.shard_map(
        body,
        mesh=mesh,
        in_specs=(rows, rows, P(), rows, rows, blocks, blocks, blocks),
        out_specs=(rows, P(AXES), rows, blocks, blocks, blocks),
        check_vma=False,
    )
```

```python
import functools

import jax
import jax.numpy as jnp
from jax import lax
from jax.experimental import pallas as pl
from jax.experimental.pallas import tpu as pltpu
from jax.sharding import PartitionSpec as P

BF = jnp.bfloat16
F32 = jnp.float32
AXES = ("seq", "expert")


def coords(outer, inner):
    s = lax.axis_index("seq")
    e = lax.axis_index("expert")
    return s, e // inner, e % inner


LANES = 128
MESH = pl.DeviceIdType.MESH


def remote(src, dst, send, recv, peer):
    return pltpu.make_async_remote_copy(
        src_ref=src, dst_ref=dst, send_sem=send, recv_sem=recv, device_id=peer, device_id_type=MESH
    )


def greet_all(s, o, i, seqs, outer, inner):
    barrier = pltpu.get_barrier_semaphore()
    plane = seqs * inner
    p = s * inner + i
    for ok, step in ((o > 0, -1), (o < outer - 1, 1)):

        @pl.when(ok)
        def _():
            pl.semaphore_signal(
                barrier, inc=1, device_id=(s, (o + step) * inner + i), device_id_type=MESH
            )

    def greet(q, carry):
        to = (p + q) % plane
        pl.semaphore_signal(
            barrier, inc=1, device_id=(to // inner, o * inner + to % inner), device_id_type=MESH
        )
        return carry

    lax.fori_loop(1, plane, greet, 0)
    beside = (o > 0).astype(jnp.int32) + (o < outer - 1).astype(jnp.int32)
    pl.semaphore_wait(barrier, plane - 1 + beside)


def dispatch_kernel(
    seqs, outer, inner, normed, cot, table, got_in, got_cot, table_all,
    line, table_line, stage_cot, stage_in, line_send, line_recv, table_send, table_recv,
    plane_send, plane_recv, own_sem, out_sem,
):
    s, o, i = coords(outer, inner)
    plane = seqs * inner
    p = s * inner + i
    width = normed.shape[1]
    cap = got_in.shape[1]
    greet_all(s, o, i, seqs, outer, inner)

    sources = (cot, normed)
    stages = (stage_cot, stage_in)
    targets = (got_cot, got_in)

    def hop(kind, src, way, own):
        peer = (s, (o + 1 - 2 * way) * inner + i)
        if kind == 2:
            held = table if own else table_line.at[src]
            return remote(held, table_line.at[src], table_send.at[src, way], table_recv.at[src], peer)
        held = sources[kind] if own else line.at[kind, src]
        return remote(
            held, line.at[kind, src], line_send.at[kind, src, way], line_recv.at[kind, src], peer
        )

    def plane_copy(t, src, q):
        to = (p + q) % plane
        home = s * (outer * inner) + src * inner + i
        return remote(
            stages[t].at[src, to], targets[t].at[home],
            plane_send.at[t, src, q], plane_recv.at[t, src, q],
            (to // inner, o * inner + to % inner),
        )

    def own_copy(t, src):
        home = s * (outer * inner) + src * inner + i
        return pltpu.make_async_copy(stages[t].at[src, p], targets[t].at[home], own_sem.at[t, src])

    def table_out(src, own):
        held = table.at[o] if own else table_line.at[src, o]
        return pltpu.make_async_copy(held, table_all.at[src], out_sem.at[src])

    def place(t, src, own):
        step = 512 if width % 512 == 0 else width
        pick = (table[o] if own else table_line[src, o]).astype(F32)
        mark = jnp.where(pick != 0.0, 1.0, 0.0).astype(BF)
        if t == 0:
            gate = jnp.broadcast_to(jnp.sum(pick, axis=1, keepdims=True), (plane * cap, LANES))
            stage_cot[src, :, :, width:] = gate.astype(BF).reshape(plane, cap, LANES)

        def part(c, carry):
            cols = pl.ds(pl.multiple_of(c * step, step), step)
            rows = sources[t][:, cols] if own else line[t, src, :, cols]
            put = jnp.dot(mark, rows, preferred_element_type=F32).astype(BF)
            stages[t][src, :, :, cols] = put.reshape(plane, cap, step)
            return carry

        lax.fori_loop(0, width // step, part, 0)
        own_copy(t, src).start()

        def push(q, carry):
            plane_copy(t, src, q).start()
            return carry

        lax.fori_loop(1, plane, push, 0)

    can_go = (o < outer - 1, o > 0)
    for kind in (2, 0, 1):
        for way in range(2):

            @pl.when(can_go[way])
            def _():
                hop(kind, o, way, True).start()

    for t in range(2):
        place(t, o, True)
    table_out(o, True).start()

    for j in range(1, outer):
        for way in range(2):
            src = o - j if way == 0 else o + j
            here = src >= 0 if way == 0 else src < outer

            @pl.when(here)
            def _():
                for kind in (2, 0, 1):
                    hop(kind, src, way, False).wait_recv()

                    @pl.when(can_go[way])
                    def _():
                        hop(kind, src, way, False).start()

                    if kind < 2:
                        place(kind, src, False)
                table_out(src, False).start()

    for kind in (2, 0, 1):
        for way in range(2):

            @pl.when(can_go[way])
            def _():
                hop(kind, o, way, True).wait_send()

                for j in range(1, outer):
                    src = o - j if way == 0 else o + j
                    here = src >= 0 if way == 0 else src < outer

                    @pl.when(here)
                    def _():
                        hop(kind, src, way, False).wait_send()

    table_out(o, True).wait()
    for j in range(1, outer):
        for way in range(2):
            src = o - j if way == 0 else o + j
            here = src >= 0 if way == 0 else src < outer

            @pl.when(here)
            def _():
                table_out(src, False).wait()

    for t in range(2):
        for src in range(outer):
            own_copy(t, src).wait()

            def finish(q, carry):
                plane_copy(t, src, q).wait_recv()
                plane_copy(t, src, q).wait_send()
                return carry

            lax.fori_loop(1, plane, finish, 0)


def dispatch(normed, cot, table, seqs, outer, inner, cap):
    rows, width = normed.shape
    plane = seqs * inner
    count = plane * outer
    vmem = pl.BlockSpec(memory_space=pltpu.VMEM)
    anywhere = pl.BlockSpec(memory_space=pl.ANY)
    dma = pltpu.SemaphoreType.DMA
    return pl.pallas_call(
        functools.partial(dispatch_kernel, seqs, outer, inner),
        out_shape=(
            jax.ShapeDtypeStruct((count, cap, width), BF),
            jax.ShapeDtypeStruct((count, cap, width + LANES), BF),
            jax.ShapeDtypeStruct(table.shape, BF),
        ),
        in_specs=[vmem, vmem, vmem],
        out_specs=(anywhere, anywhere, anywhere),
        scratch_shapes=[
            pltpu.VMEM((2, outer, rows, width), BF),
            pltpu.VMEM((outer,) + table.shape, BF),
            pltpu.VMEM((outer, plane, cap, width + LANES), BF),
            pltpu.VMEM((outer, plane, cap, width), BF),
            dma((2, outer, 2)),
            dma((2, outer)),
            dma((outer, 2)),
            dma((outer,)),
            dma((2, outer, plane)),
            dma((2, outer, plane)),
            dma((2, outer)),
            dma((outer,)),
        ],
        compiler_params=pltpu.CompilerParams(
            collective_id=0, has_side_effects=True, vmem_limit_bytes=40 * 1024 * 1024
        ),
        name="dispatch",
    )(normed, cot, table)


def expert_backward(rows_in, rows_cot, rows_gate, gate_w, up_w, down_w):
    pre_gate = jnp.dot(rows_in, gate_w, preferred_element_type=F32)
    pre_up = jnp.dot(rows_in, up_w, preferred_element_type=F32)
    sigmoid_gate = jax.nn.sigmoid(pre_gate)
    silu_gate = pre_gate * sigmoid_gate
    act = (silu_gate * pre_up).astype(BF)
    expert_out = jnp.dot(act, down_w, preferred_element_type=F32)
    slot_grad = jnp.sum(rows_cot.astype(F32) * expert_out, axis=1).astype(BF)
    d_expert = (rows_gate.astype(F32)[:, None] * rows_cot.astype(F32)).astype(BF)
    d_act = lax.dot_general(d_expert, down_w, (((1,), (1,)), ((), ())), preferred_element_type=F32)
    grad_gate = (d_act * pre_up * sigmoid_gate * (1.0 + pre_gate * (1.0 - sigmoid_gate))).astype(BF)
    grad_up = (d_act * silu_gate).astype(BF)
    turned = (((0,), (0,)), ((), ()))
    grad_down_w = lax.dot_general(act, d_expert, turned, preferred_element_type=F32).astype(BF)
    grad_gate_w = lax.dot_general(rows_in, grad_gate, turned, preferred_element_type=F32).astype(BF)
    grad_up_w = lax.dot_general(rows_in, grad_up, turned, preferred_element_type=F32).astype(BF)
    across = (((1,), (1,)), ((), ()))
    d_rows = (
        lax.dot_general(grad_gate, gate_w, across, preferred_element_type=F32)
        + lax.dot_general(grad_up, up_w, across, preferred_element_type=F32)
    ).astype(BF)
    return (d_rows, slot_grad, grad_gate_w, grad_up_w, grad_down_w)


def body(hidden_in, d_output, gain, route_ids, gates, w_gate, w_up, w_down):
    tok_rows, width = hidden_in.shape
    top_count = route_ids.shape[1]
    seqs = lax.axis_size("seq")
    per_seq = lax.axis_size("expert")
    outer = 4 if per_seq % 4 == 0 else 2
    inner = per_seq // outer
    devices = seqs * per_seq
    experts = w_gate.shape[0] * devices
    capacity = max(2, tok_rows * top_count * 3 // (2 * experts))
    cap = -(-capacity // 8) * 8
    wide_rows = hidden_in.astype(F32)
    inverse_rms = lax.rsqrt(jnp.mean(wide_rows * wide_rows, axis=1, keepdims=True) + 1e-06)
    unit_rows = wide_rows * inverse_rms
    normed = (unit_rows * gain[None, :]).astype(BF)

    ids_t = route_ids.T
    gates_t = gates.T
    names = jnp.arange(experts, dtype=jnp.int32)
    hit = ids_t[:, None, :] == names[None, :, None]
    chosen = jnp.any(hit, axis=0)
    gate_map = jnp.sum(jnp.where(hit, gates_t[:, None, :].astype(F32), 0.0), axis=0)
    token = jnp.arange(tok_rows, dtype=jnp.int32)
    earlier = (token[:, None] < token[None, :]).astype(BF)
    position = jnp.dot(chosen.astype(BF), earlier, preferred_element_type=F32).astype(jnp.int32)
    placed = chosen[:, None, :] & (position[:, None, :] == jnp.arange(cap, dtype=jnp.int32)[None, :, None])
    table = placed.astype(BF)
    gate_table = jnp.where(placed, gate_map[:, None, :], 0.0).astype(BF)
    by_plane = (
        gate_table.reshape(seqs, outer, inner, cap, tok_rows)
        .transpose(1, 0, 2, 3, 4)
        .reshape(outer, seqs * inner * cap, tok_rows)
    )
    got_in, got_cot, _ = dispatch(normed, d_output, by_plane, seqs, outer, inner, cap)
    d_rows, slot_grad, grad_gate_w, grad_up_w, grad_down_w = expert_backward(
        got_in.reshape(-1, width), got_cot[:, :, :width].reshape(-1, width),
        got_cot[:, :, width].reshape(-1),
        w_gate[0], w_up[0], w_down[0],
    )
    back = jnp.concatenate(
        [d_rows, jnp.broadcast_to(slot_grad[:, None], (slot_grad.shape[0], LANES))], axis=1
    ).reshape(devices, cap, width + LANES)
    home = lax.all_to_all(back, AXES, split_axis=0, concat_axis=0, tiled=True)
    home_rows = home[:, :, :width]
    home_grad = home[:, :, width]
    d_normed = lax.dot_general(
        table.reshape(-1, tok_rows), home_rows.reshape(-1, width), (((0,), (0,)), ((), ())),
        preferred_element_type=F32,
    )
    grad_map = jnp.sum(jnp.where(placed, home_grad[:, :, None].astype(F32), 0.0), axis=1)
    d_gates = jnp.sum(jnp.where(hit, grad_map[None], 0.0), axis=1).astype(BF).T
    gain_term = jnp.sum(d_normed * unit_rows, axis=0)
    gain_parts = lax.all_to_all(
        gain_term.reshape(devices, -1), AXES, split_axis=0, concat_axis=0, tiled=True
    )
    d_gain = jnp.sum(gain_parts, axis=0)
    d_unit = d_normed * gain[None, :]
    inner_mean = jnp.mean(d_unit * unit_rows, axis=1, keepdims=True)
    d_hidden_in = (
        d_output.astype(F32) + inverse_rms * (d_unit - unit_rows * inner_mean)
    ).astype(BF)
    return (d_hidden_in, d_gain, d_gates, grad_gate_w[None], grad_up_w[None], grad_down_w[None])


def solution(mesh):
    rows = P(AXES, None)
    blocks = P(AXES, None, None)
    return jax.shard_map(
        body,
        mesh=mesh,
        in_specs=(rows, rows, P(), rows, rows, blocks, blocks, blocks),
        out_specs=(rows, P(AXES), rows, blocks, blocks, blocks),
        check_vma=False,
    )
```

```python
import functools

import jax
import jax.numpy as jnp
from jax import lax
from jax.experimental import pallas as pl
from jax.experimental.pallas import tpu as pltpu
from jax.sharding import PartitionSpec as P

BF = jnp.bfloat16
F32 = jnp.float32
AXES = ("seq", "expert")


def coords(outer, inner):
    s = lax.axis_index("seq")
    e = lax.axis_index("expert")
    return s, e // inner, e % inner


LANES = 128
MESH = pl.DeviceIdType.MESH


def remote(src, dst, send, recv, peer):
    return pltpu.make_async_remote_copy(
        src_ref=src, dst_ref=dst, send_sem=send, recv_sem=recv, device_id=peer, device_id_type=MESH
    )


def greet_all(s, o, i, seqs, outer, inner):
    barrier = pltpu.get_barrier_semaphore()
    plane = seqs * inner
    p = s * inner + i
    for ok, step in ((o > 0, -1), (o < outer - 1, 1)):

        @pl.when(ok)
        def _():
            pl.semaphore_signal(
                barrier, inc=1, device_id=(s, (o + step) * inner + i), device_id_type=MESH
            )

    def greet(q, carry):
        to = (p + q) % plane
        pl.semaphore_signal(
            barrier, inc=1, device_id=(to // inner, o * inner + to % inner), device_id_type=MESH
        )
        return carry

    lax.fori_loop(1, plane, greet, 0)
    beside = (o > 0).astype(jnp.int32) + (o < outer - 1).astype(jnp.int32)
    pl.semaphore_wait(barrier, plane - 1 + beside)


def dispatch_kernel(
    seqs, outer, inner, normed, cot, table, got_in, got_cot, table_all,
    line, table_line, stage_cot, stage_in, line_send, line_recv, table_send, table_recv,
    plane_send, plane_recv, own_sem, out_sem,
):
    s, o, i = coords(outer, inner)
    plane = seqs * inner
    p = s * inner + i
    width = normed.shape[1]
    cap = got_in.shape[1]
    greet_all(s, o, i, seqs, outer, inner)

    sources = (cot, normed)
    stages = (stage_cot, stage_in)
    targets = (got_cot, got_in)

    def hop(kind, src, way, own):
        peer = (s, (o + 1 - 2 * way) * inner + i)
        if kind == 2:
            held = table if own else table_line.at[src]
            return remote(held, table_line.at[src], table_send.at[src, way], table_recv.at[src], peer)
        held = sources[kind] if own else line.at[kind, src]
        return remote(
            held, line.at[kind, src], line_send.at[kind, src, way], line_recv.at[kind, src], peer
        )

    def plane_copy(t, src, q):
        to = (p + q) % plane
        home = s * (outer * inner) + src * inner + i
        return remote(
            stages[t].at[src, to], targets[t].at[home],
            plane_send.at[t, src, q], plane_recv.at[t, src, q],
            (to // inner, o * inner + to % inner),
        )

    def own_copy(t, src):
        home = s * (outer * inner) + src * inner + i
        return pltpu.make_async_copy(stages[t].at[src, p], targets[t].at[home], own_sem.at[t, src])

    def table_out(src, own):
        held = table.at[o] if own else table_line.at[src, o]
        return pltpu.make_async_copy(held, table_all.at[src], out_sem.at[src])

    def place(t, src, own):
        step = 512 if width % 512 == 0 else width
        pick = (table[o] if own else table_line[src, o]).astype(F32)
        mark = jnp.where(pick != 0.0, 1.0, 0.0).astype(BF)
        if t == 0:
            gate = jnp.broadcast_to(jnp.sum(pick, axis=1, keepdims=True), (plane * cap, LANES))
            stage_cot[src, :, :, width:] = gate.astype(BF).reshape(plane, cap, LANES)

        def part(c, carry):
            cols = pl.ds(pl.multiple_of(c * step, step), step)
            rows = sources[t][:, cols] if own else line[t, src, :, cols]
            put = jnp.dot(mark, rows, preferred_element_type=F32).astype(BF)
            stages[t][src, :, :, cols] = put.reshape(plane, cap, step)
            return carry

        lax.fori_loop(0, width // step, part, 0)
        own_copy(t, src).start()

        def push(q, carry):
            plane_copy(t, src, q).start()
            return carry

        lax.fori_loop(1, plane, push, 0)

    can_go = (o < outer - 1, o > 0)
    for kind in (2, 0, 1):
        for way in range(2):

            @pl.when(can_go[way])
            def _():
                hop(kind, o, way, True).start()

    for t in range(2):
        place(t, o, True)
    table_out(o, True).start()

    for j in range(1, outer):
        for way in range(2):
            src = o - j if way == 0 else o + j
            here = src >= 0 if way == 0 else src < outer

            @pl.when(here)
            def _():
                for kind in (2, 0, 1):
                    hop(kind, src, way, False).wait_recv()

                    @pl.when(can_go[way])
                    def _():
                        hop(kind, src, way, False).start()

                    if kind < 2:
                        place(kind, src, False)
                table_out(src, False).start()

    for kind in (2, 0, 1):
        for way in range(2):

            @pl.when(can_go[way])
            def _():
                hop(kind, o, way, True).wait_send()

                for j in range(1, outer):
                    src = o - j if way == 0 else o + j
                    here = src >= 0 if way == 0 else src < outer

                    @pl.when(here)
                    def _():
                        hop(kind, src, way, False).wait_send()

    table_out(o, True).wait()
    for j in range(1, outer):
        for way in range(2):
            src = o - j if way == 0 else o + j
            here = src >= 0 if way == 0 else src < outer

            @pl.when(here)
            def _():
                table_out(src, False).wait()

    for t in range(2):
        for src in range(outer):
            own_copy(t, src).wait()

            def finish(q, carry):
                plane_copy(t, src, q).wait_recv()
                plane_copy(t, src, q).wait_send()
                return carry

            lax.fori_loop(1, plane, finish, 0)


def dispatch(normed, cot, table, seqs, outer, inner, cap):
    rows, width = normed.shape
    plane = seqs * inner
    count = plane * outer
    vmem = pl.BlockSpec(memory_space=pltpu.VMEM)
    anywhere = pl.BlockSpec(memory_space=pl.ANY)
    dma = pltpu.SemaphoreType.DMA
    return pl.pallas_call(
        functools.partial(dispatch_kernel, seqs, outer, inner),
        out_shape=(
            jax.ShapeDtypeStruct((count, cap, width), BF),
            jax.ShapeDtypeStruct((count, cap, width + LANES), BF),
            jax.ShapeDtypeStruct(table.shape, BF),
        ),
        in_specs=[vmem, vmem, vmem],
        out_specs=(anywhere, anywhere, anywhere),
        scratch_shapes=[
            pltpu.VMEM((2, outer, rows, width), BF),
            pltpu.VMEM((outer,) + table.shape, BF),
            pltpu.VMEM((outer, plane, cap, width + LANES), BF),
            pltpu.VMEM((outer, plane, cap, width), BF),
            dma((2, outer, 2)),
            dma((2, outer)),
            dma((outer, 2)),
            dma((outer,)),
            dma((2, outer, plane)),
            dma((2, outer, plane)),
            dma((2, outer)),
            dma((outer,)),
        ],
        compiler_params=pltpu.CompilerParams(
            collective_id=0, has_side_effects=True, vmem_limit_bytes=40 * 1024 * 1024
        ),
        name="dispatch",
    )(normed, cot, table)


def collect_kernel(
    seqs, outer, inner, back, table, out_rows, out_grad,
    landed, running, stage, plane_send, plane_recv, own_sem, run_send, run_recv,
):
    s, o, i = coords(outer, inner)
    plane = seqs * inner
    p = s * inner + i
    cap = landed.shape[2]
    wide = landed.shape[3]
    width = wide - LANES
    greet_all(s, o, i, seqs, outer, inner)

    def plane_copy(src, q):
        to = (p + q) % plane
        home = (to // inner) * (outer * inner) + src * inner + to % inner
        return remote(
            back.at[home], landed.at[src, p], plane_send.at[src, q], plane_recv.at[src, q],
            (to // inner, o * inner + to % inner),
        )

    def own_copy(src):
        home = s * (outer * inner) + src * inner + i
        return pltpu.make_async_copy(back.at[home], landed.at[src, p], own_sem.at[src])

    def run_copy(src, way):
        peer = (s, (o - 1 + 2 * way) * inner + i)
        return remote(
            stage.at[src], running.at[src, way], run_send.at[src, way], run_recv.at[src, way], peer
        )

    def cases(j):
        return ((o - j, o - j >= 0, 0), (o + j, o + j < outer, 1))

    def push_all(src):
        own_copy(src).start()

        def push(q, carry):
            plane_copy(src, q).start()
            return carry

        lax.fori_loop(1, plane, push, 0)

    def await_all(src):
        own_copy(src).wait()

        def wait(q, carry):
            plane_copy(src, q).wait_recv()
            return carry

        lax.fori_loop(1, plane, wait, 0)

    turned = (((0,), (0,)), ((), ()))

    def marks(src):
        return jnp.where(table[src].astype(F32) != 0.0, 1.0, 0.0).astype(BF)

    def sums(src, cols, size):
        values = landed[src, :, :, cols].reshape(plane * cap, size)
        return lax.dot_general(marks(src), values, turned, preferred_element_type=F32)

    def grads(src):
        values = landed[src, :, :, width:].astype(F32)
        column = lax.broadcasted_iota(jnp.int32, values.shape, 2)
        expert = o * plane + lax.broadcasted_iota(jnp.int32, values.shape, 0)
        values = jnp.where(column == expert, values, 0.0).reshape(plane * cap, LANES).astype(BF)
        return lax.dot_general(marks(src), values, turned, preferred_element_type=F32)

    step = 512 if width % 512 == 0 else width

    def each(part):
        def one(c, carry):
            part(pl.ds(pl.multiple_of(c * step, step), step))
            return carry

        lax.fori_loop(0, width // step, one, 0)

    for j in range(outer - 1, 0, -1):
        for src, here, way in cases(j):

            @pl.when(here)
            def _():
                push_all(src)

    push_all(o)

    more = (o < outer - 1, o > 0)
    for j in range(outer - 1, 0, -1):
        for src, here, way in cases(j):

            @pl.when(here)
            def _():
                await_all(src)

                def first(cols):
                    stage[src, :, cols] = sums(src, cols, step).astype(BF)

                def later(cols):
                    total = sums(src, cols, step) + running[src, way, :, cols].astype(F32)
                    stage[src, :, cols] = total.astype(BF)

                @pl.when(more[way])
                def _():
                    run_copy(src, way).wait_recv()
                    each(later)
                    total = grads(src) + running[src, way, :, width:].astype(F32)
                    stage[src, :, width:] = total.astype(BF)

                @pl.when(jnp.logical_not(more[way]))
                def _():
                    each(first)
                    stage[src, :, width:] = grads(src).astype(BF)

                run_copy(src, way).start()

    await_all(o)

    def mine(cols):
        out_rows[:, cols] = sums(o, cols, step)

    each(mine)
    out_grad[...] = grads(o)
    for way in range(2):

        @pl.when(more[way])
        def _():
            run_copy(o, way).wait_recv()

            def add(cols):
                out_rows[:, cols] = out_rows[:, cols] + running[o, way, :, cols].astype(F32)

            each(add)
            out_grad[...] = out_grad[...] + running[o, way, :, width:].astype(F32)

    for j in range(1, outer):
        for src, here, way in cases(j):

            @pl.when(here)
            def _():
                run_copy(src, way).wait_send()

    for src in range(outer):

        def finish(q, carry):
            plane_copy(src, q).wait_send()
            return carry

        lax.fori_loop(1, plane, finish, 0)


def collect(back, table, seqs, outer, inner):
    count, cap, wide = back.shape
    plane = seqs * inner
    rows = table.shape[2]
    vmem = pl.BlockSpec(memory_space=pltpu.VMEM)
    dma = pltpu.SemaphoreType.DMA
    return pl.pallas_call(
        functools.partial(collect_kernel, seqs, outer, inner),
        out_shape=(
            jax.ShapeDtypeStruct((rows, wide - LANES), F32),
            jax.ShapeDtypeStruct((rows, LANES), F32),
        ),
        in_specs=[pl.BlockSpec(memory_space=pl.ANY), vmem],
        out_specs=(vmem, vmem),
        scratch_shapes=[
            pltpu.VMEM((outer, plane, cap, wide), BF),
            pltpu.VMEM((outer, 2, rows, wide), BF),
            pltpu.VMEM((outer, rows, wide), BF),
            dma((outer, plane)),
            dma((outer, plane)),
            dma((outer,)),
            dma((outer, 2)),
            dma((outer, 2)),
        ],
        compiler_params=pltpu.CompilerParams(
            collective_id=1, has_side_effects=True, vmem_limit_bytes=40 * 1024 * 1024
        ),
        name="collect",
    )(back, table)


def expert_backward(rows_in, rows_cot, rows_gate, gate_w, up_w, down_w):
    pre_gate = jnp.dot(rows_in, gate_w, preferred_element_type=F32)
    pre_up = jnp.dot(rows_in, up_w, preferred_element_type=F32)
    sigmoid_gate = jax.nn.sigmoid(pre_gate)
    silu_gate = pre_gate * sigmoid_gate
    act = (silu_gate * pre_up).astype(BF)
    expert_out = jnp.dot(act, down_w, preferred_element_type=F32)
    slot_grad = jnp.sum(rows_cot.astype(F32) * expert_out, axis=1).astype(BF)
    d_expert = (rows_gate.astype(F32)[:, None] * rows_cot.astype(F32)).astype(BF)
    d_act = lax.dot_general(d_expert, down_w, (((1,), (1,)), ((), ())), preferred_element_type=F32)
    grad_gate = (d_act * pre_up * sigmoid_gate * (1.0 + pre_gate * (1.0 - sigmoid_gate))).astype(BF)
    grad_up = (d_act * silu_gate).astype(BF)
    turned = (((0,), (0,)), ((), ()))
    grad_down_w = lax.dot_general(act, d_expert, turned, preferred_element_type=F32).astype(BF)
    grad_gate_w = lax.dot_general(rows_in, grad_gate, turned, preferred_element_type=F32).astype(BF)
    grad_up_w = lax.dot_general(rows_in, grad_up, turned, preferred_element_type=F32).astype(BF)
    across = (((1,), (1,)), ((), ()))
    d_rows = (
        lax.dot_general(grad_gate, gate_w, across, preferred_element_type=F32)
        + lax.dot_general(grad_up, up_w, across, preferred_element_type=F32)
    ).astype(BF)
    return (d_rows, slot_grad, grad_gate_w, grad_up_w, grad_down_w)


def body(hidden_in, d_output, gain, route_ids, gates, w_gate, w_up, w_down):
    tok_rows, width = hidden_in.shape
    top_count = route_ids.shape[1]
    seqs = lax.axis_size("seq")
    per_seq = lax.axis_size("expert")
    outer = 4 if per_seq % 4 == 0 else 2
    inner = per_seq // outer
    devices = seqs * per_seq
    experts = w_gate.shape[0] * devices
    capacity = max(2, tok_rows * top_count * 3 // (2 * experts))
    cap = -(-capacity // 8) * 8
    wide_rows = hidden_in.astype(F32)
    inverse_rms = lax.rsqrt(jnp.mean(wide_rows * wide_rows, axis=1, keepdims=True) + 1e-06)
    unit_rows = wide_rows * inverse_rms
    normed = (unit_rows * gain[None, :]).astype(BF)

    ids_t = route_ids.T
    gates_t = gates.T
    names = jnp.arange(experts, dtype=jnp.int32)
    hit = ids_t[:, None, :] == names[None, :, None]
    chosen = jnp.any(hit, axis=0)
    gate_map = jnp.sum(jnp.where(hit, gates_t[:, None, :].astype(F32), 0.0), axis=0)
    token = jnp.arange(tok_rows, dtype=jnp.int32)
    earlier = (token[:, None] < token[None, :]).astype(BF)
    position = jnp.dot(chosen.astype(BF), earlier, preferred_element_type=F32).astype(jnp.int32)
    placed = chosen[:, None, :] & (position[:, None, :] == jnp.arange(cap, dtype=jnp.int32)[None, :, None])
    table = placed.astype(BF)
    gate_table = jnp.where(placed, gate_map[:, None, :], 0.0).astype(BF)
    by_plane = (
        gate_table.reshape(seqs, outer, inner, cap, tok_rows)
        .transpose(1, 0, 2, 3, 4)
        .reshape(outer, seqs * inner * cap, tok_rows)
    )
    got_in, got_cot, tables = dispatch(normed, d_output, by_plane, seqs, outer, inner, cap)
    d_rows, slot_grad, grad_gate_w, grad_up_w, grad_down_w = expert_backward(
        got_in.reshape(-1, width), got_cot[:, :, :width].reshape(-1, width),
        got_cot[:, :, width].reshape(-1),
        w_gate[0], w_up[0], w_down[0],
    )
    back = jnp.concatenate(
        [d_rows, jnp.broadcast_to(slot_grad[:, None], (slot_grad.shape[0], LANES))], axis=1
    ).reshape(devices, cap, width + LANES)
    d_normed, grad_map = collect(back, tables, seqs, outer, inner)
    lane = jnp.arange(LANES, dtype=jnp.int32)
    ids_column = (
        route_ids // inner % outer * (seqs * inner) + route_ids // per_seq * inner + route_ids % inner
    )
    d_gates = jnp.sum(
        jnp.where(ids_column[:, :, None] == lane[None, None, :], grad_map[:, None, :], 0.0), axis=2
    ).astype(BF)
    gain_term = jnp.sum(d_normed * unit_rows, axis=0)
    gain_parts = lax.all_to_all(
        gain_term.reshape(devices, -1), AXES, split_axis=0, concat_axis=0, tiled=True
    )
    d_gain = jnp.sum(gain_parts, axis=0)
    d_unit = d_normed * gain[None, :]
    inner_mean = jnp.mean(d_unit * unit_rows, axis=1, keepdims=True)
    d_hidden_in = (
        d_output.astype(F32) + inverse_rms * (d_unit - unit_rows * inner_mean)
    ).astype(BF)
    return (d_hidden_in, d_gain, d_gates, grad_gate_w[None], grad_up_w[None], grad_down_w[None])


def solution(mesh):
    rows = P(AXES, None)
    blocks = P(AXES, None, None)
    return jax.shard_map(
        body,
        mesh=mesh,
        in_specs=(rows, rows, P(), rows, rows, blocks, blocks, blocks),
        out_specs=(rows, P(AXES), rows, blocks, blocks, blocks),
        check_vma=False,
    )
```

```python
import functools

import jax
import jax.numpy as jnp
from jax import lax
from jax.experimental import pallas as pl
from jax.experimental.pallas import tpu as pltpu
from jax.sharding import PartitionSpec as P

BF = jnp.bfloat16
F32 = jnp.float32
AXES = ("seq", "expert")


def coords(outer, inner):
    s = lax.axis_index("seq")
    e = lax.axis_index("expert")
    return s, e // inner, e % inner


LANES = 128
MESH = pl.DeviceIdType.MESH


def remote(src, dst, send, recv, peer):
    return pltpu.make_async_remote_copy(
        src_ref=src, dst_ref=dst, send_sem=send, recv_sem=recv, device_id=peer, device_id_type=MESH
    )


def greet_all(s, o, i, seqs, outer, inner):
    barrier = pltpu.get_barrier_semaphore()
    plane = seqs * inner
    p = s * inner + i
    for ok, step in ((o > 0, -1), (o < outer - 1, 1)):

        @pl.when(ok)
        def _():
            pl.semaphore_signal(
                barrier, inc=1, device_id=(s, (o + step) * inner + i), device_id_type=MESH
            )

    def greet(q, carry):
        to = (p + q) % plane
        pl.semaphore_signal(
            barrier, inc=1, device_id=(to // inner, o * inner + to % inner), device_id_type=MESH
        )
        return carry

    lax.fori_loop(1, plane, greet, 0)
    beside = (o > 0).astype(jnp.int32) + (o < outer - 1).astype(jnp.int32)
    pl.semaphore_wait(barrier, plane - 1 + beside)


def dispatch_kernel(
    seqs, outer, inner, normed, cot, table, got_in, got_cot, table_all,
    line, table_line, stage_cot, stage_in, line_send, line_recv, table_send, table_recv,
    plane_send, plane_recv, own_sem, out_sem,
):
    s, o, i = coords(outer, inner)
    plane = seqs * inner
    p = s * inner + i
    width = normed.shape[1]
    cap = got_in.shape[1]
    greet_all(s, o, i, seqs, outer, inner)

    sources = (cot, normed)
    stages = (stage_cot, stage_in)
    targets = (got_cot, got_in)

    def hop(kind, src, way, own):
        peer = (s, (o + 1 - 2 * way) * inner + i)
        if kind == 2:
            held = table if own else table_line.at[src]
            return remote(held, table_line.at[src], table_send.at[src, way], table_recv.at[src], peer)
        held = sources[kind] if own else line.at[kind, src]
        return remote(
            held, line.at[kind, src], line_send.at[kind, src, way], line_recv.at[kind, src], peer
        )

    def plane_copy(t, src, q):
        to = (p + q) % plane
        home = s * (outer * inner) + src * inner + i
        return remote(
            stages[t].at[src, to], targets[t].at[home],
            plane_send.at[t, src, q], plane_recv.at[t, src, q],
            (to // inner, o * inner + to % inner),
        )

    def own_copy(t, src):
        home = s * (outer * inner) + src * inner + i
        return pltpu.make_async_copy(stages[t].at[src, p], targets[t].at[home], own_sem.at[t, src])

    def table_out(src, own):
        held = table.at[o] if own else table_line.at[src, o]
        return pltpu.make_async_copy(held, table_all.at[src], out_sem.at[src])

    def place(t, src, own):
        step = 512 if width % 512 == 0 else width
        pick = (table[o] if own else table_line[src, o]).astype(F32)
        mark = jnp.where(pick != 0.0, 1.0, 0.0).astype(BF)
        if t == 0:
            gate = jnp.broadcast_to(jnp.sum(pick, axis=1, keepdims=True), (plane * cap, LANES))
            stage_cot[src, :, :, width:] = gate.astype(BF).reshape(plane, cap, LANES)

        def part(c, carry):
            cols = pl.ds(pl.multiple_of(c * step, step), step)
            rows = sources[t][:, cols] if own else line[t, src, :, cols]
            put = jnp.dot(mark, rows, preferred_element_type=F32).astype(BF)
            stages[t][src, :, :, cols] = put.reshape(plane, cap, step)
            return carry

        lax.fori_loop(0, width // step, part, 0)
        own_copy(t, src).start()

        def push(q, carry):
            plane_copy(t, src, q).start()
            return carry

        lax.fori_loop(1, plane, push, 0)

    can_go = (o < outer - 1, o > 0)
    for kind in (2, 0, 1):
        for way in range(2):

            @pl.when(can_go[way])
            def _():
                hop(kind, o, way, True).start()

    for t in range(2):
        place(t, o, True)
    table_out(o, True).start()

    for j in range(1, outer):
        for way in range(2):
            src = o - j if way == 0 else o + j
            here = src >= 0 if way == 0 else src < outer

            @pl.when(here)
            def _():
                for kind in (2, 0, 1):
                    hop(kind, src, way, False).wait_recv()

                    @pl.when(can_go[way])
                    def _():
                        hop(kind, src, way, False).start()

                    if kind < 2:
                        place(kind, src, False)
                table_out(src, False).start()

    for kind in (2, 0, 1):
        for way in range(2):

            @pl.when(can_go[way])
            def _():
                hop(kind, o, way, True).wait_send()

                for j in range(1, outer):
                    src = o - j if way == 0 else o + j
                    here = src >= 0 if way == 0 else src < outer

                    @pl.when(here)
                    def _():
                        hop(kind, src, way, False).wait_send()

    table_out(o, True).wait()
    for j in range(1, outer):
        for way in range(2):
            src = o - j if way == 0 else o + j
            here = src >= 0 if way == 0 else src < outer

            @pl.when(here)
            def _():
                table_out(src, False).wait()

    for t in range(2):
        for src in range(outer):
            own_copy(t, src).wait()

            def finish(q, carry):
                plane_copy(t, src, q).wait_recv()
                plane_copy(t, src, q).wait_send()
                return carry

            lax.fori_loop(1, plane, finish, 0)


def dispatch(normed, cot, table, seqs, outer, inner, cap):
    rows, width = normed.shape
    plane = seqs * inner
    count = plane * outer
    vmem = pl.BlockSpec(memory_space=pltpu.VMEM)
    anywhere = pl.BlockSpec(memory_space=pl.ANY)
    dma = pltpu.SemaphoreType.DMA
    return pl.pallas_call(
        functools.partial(dispatch_kernel, seqs, outer, inner),
        out_shape=(
            jax.ShapeDtypeStruct((count, cap, width), BF),
            jax.ShapeDtypeStruct((count, cap, width + LANES), BF),
            jax.ShapeDtypeStruct(table.shape, BF),
        ),
        in_specs=[vmem, vmem, vmem],
        out_specs=(anywhere, anywhere, anywhere),
        scratch_shapes=[
            pltpu.VMEM((2, outer, rows, width), BF),
            pltpu.VMEM((outer,) + table.shape, BF),
            pltpu.VMEM((outer, plane, cap, width + LANES), BF),
            pltpu.VMEM((outer, plane, cap, width), BF),
            dma((2, outer, 2)),
            dma((2, outer)),
            dma((outer, 2)),
            dma((outer,)),
            dma((2, outer, plane)),
            dma((2, outer, plane)),
            dma((2, outer)),
            dma((outer,)),
        ],
        compiler_params=pltpu.CompilerParams(
            collective_id=0, has_side_effects=True, vmem_limit_bytes=40 * 1024 * 1024
        ),
        name="dispatch",
    )(normed, cot, table)


def collect_kernel(
    seqs, outer, inner, back, table, rows_in, grad_gate, grad_up, act, d_expert,
    out_rows, out_grad, gate_out, up_out, down_out,
    landed, running, stage, plane_send, plane_recv, own_sem, run_send, run_recv,
):
    s, o, i = coords(outer, inner)
    plane = seqs * inner
    p = s * inner + i
    cap = landed.shape[2]
    wide = landed.shape[3]
    width = wide - LANES
    greet_all(s, o, i, seqs, outer, inner)

    def plane_copy(src, q):
        to = (p + q) % plane
        home = (to // inner) * (outer * inner) + src * inner + to % inner
        return remote(
            back.at[home], landed.at[src, p], plane_send.at[src, q], plane_recv.at[src, q],
            (to // inner, o * inner + to % inner),
        )

    def own_copy(src):
        home = s * (outer * inner) + src * inner + i
        return pltpu.make_async_copy(back.at[home], landed.at[src, p], own_sem.at[src])

    def run_copy(src, way):
        peer = (s, (o - 1 + 2 * way) * inner + i)
        return remote(
            stage.at[src], running.at[src, way], run_send.at[src, way], run_recv.at[src, way], peer
        )

    def cases(j):
        return ((o - j, o - j >= 0, 0), (o + j, o + j < outer, 1))

    def push_all(src):
        own_copy(src).start()

        def push(q, carry):
            plane_copy(src, q).start()
            return carry

        lax.fori_loop(1, plane, push, 0)

    def await_all(src):
        own_copy(src).wait()

        def wait(q, carry):
            plane_copy(src, q).wait_recv()
            return carry

        lax.fori_loop(1, plane, wait, 0)

    turned = (((0,), (0,)), ((), ()))

    def marks(src):
        return jnp.where(table[src].astype(F32) != 0.0, 1.0, 0.0).astype(BF)

    def sums(src, cols, size):
        values = landed[src, :, :, cols].reshape(plane * cap, size)
        return lax.dot_general(marks(src), values, turned, preferred_element_type=F32)

    def grads(src):
        values = landed[src, :, :, width:].astype(F32)
        column = lax.broadcasted_iota(jnp.int32, values.shape, 2)
        expert = o * plane + lax.broadcasted_iota(jnp.int32, values.shape, 0)
        values = jnp.where(column == expert, values, 0.0).reshape(plane * cap, LANES).astype(BF)
        return lax.dot_general(marks(src), values, turned, preferred_element_type=F32)

    step = 512 if width % 512 == 0 else width

    def each(part):
        def one(c, carry):
            part(pl.ds(pl.multiple_of(c * step, step), step))
            return carry

        lax.fori_loop(0, width // step, one, 0)

    for j in range(outer - 1, 0, -1):
        for src, here, way in cases(j):

            @pl.when(here)
            def _():
                push_all(src)

    push_all(o)

    def weights(left, right, out):
        size = 256 if left.shape[1] % 256 == 0 else left.shape[1]

        def one(c, carry):
            cols = pl.ds(pl.multiple_of(c * size, size), size)
            out[cols, :] = lax.dot_general(
                left[:, cols], right[...], turned, preferred_element_type=F32
            ).astype(BF)
            return carry

        lax.fori_loop(0, left.shape[1] // size, one, 0)

    work = [(rows_in, grad_gate, gate_out), (rows_in, grad_up, up_out), (act, d_expert, down_out)]
    more = (o < outer - 1, o > 0)
    for j in range(outer - 1, 0, -1):
        if work:
            weights(*work.pop(0))
        for src, here, way in cases(j):

            @pl.when(here)
            def _():
                await_all(src)

                def first(cols):
                    stage[src, :, cols] = sums(src, cols, step).astype(BF)

                def later(cols):
                    total = sums(src, cols, step) + running[src, way, :, cols].astype(F32)
                    stage[src, :, cols] = total.astype(BF)

                @pl.when(more[way])
                def _():
                    run_copy(src, way).wait_recv()
                    each(later)
                    total = grads(src) + running[src, way, :, width:].astype(F32)
                    stage[src, :, width:] = total.astype(BF)

                @pl.when(jnp.logical_not(more[way]))
                def _():
                    each(first)
                    stage[src, :, width:] = grads(src).astype(BF)

                run_copy(src, way).start()

    while work:
        weights(*work.pop(0))
    await_all(o)

    def mine(cols):
        out_rows[:, cols] = sums(o, cols, step)

    each(mine)
    out_grad[...] = grads(o)
    for way in range(2):

        @pl.when(more[way])
        def _():
            run_copy(o, way).wait_recv()

            def add(cols):
                out_rows[:, cols] = out_rows[:, cols] + running[o, way, :, cols].astype(F32)

            each(add)
            out_grad[...] = out_grad[...] + running[o, way, :, width:].astype(F32)

    for j in range(1, outer):
        for src, here, way in cases(j):

            @pl.when(here)
            def _():
                run_copy(src, way).wait_send()

    for src in range(outer):

        def finish(q, carry):
            plane_copy(src, q).wait_send()
            return carry

        lax.fori_loop(1, plane, finish, 0)


def collect(back, table, parts, seqs, outer, inner):
    count, cap, wide = back.shape
    plane = seqs * inner
    rows = table.shape[2]
    vmem = pl.BlockSpec(memory_space=pltpu.VMEM)
    dma = pltpu.SemaphoreType.DMA
    return pl.pallas_call(
        functools.partial(collect_kernel, seqs, outer, inner),
        out_shape=(
            jax.ShapeDtypeStruct((rows, wide - LANES), F32),
            jax.ShapeDtypeStruct((rows, LANES), F32),
        ) + tuple(
            jax.ShapeDtypeStruct((a.shape[1], b.shape[1]), BF)
            for a, b in ((parts[0], parts[1]), (parts[0], parts[2]), (parts[3], parts[4]))
        ),
        in_specs=[pl.BlockSpec(memory_space=pl.ANY)] + [vmem] * 6,
        out_specs=(vmem,) * 5,
        scratch_shapes=[
            pltpu.VMEM((outer, plane, cap, wide), BF),
            pltpu.VMEM((outer, 2, rows, wide), BF),
            pltpu.VMEM((outer, rows, wide), BF),
            dma((outer, plane)),
            dma((outer, plane)),
            dma((outer,)),
            dma((outer, 2)),
            dma((outer, 2)),
        ],
        compiler_params=pltpu.CompilerParams(
            collective_id=1, has_side_effects=True, vmem_limit_bytes=56 * 1024 * 1024
        ),
        name="collect",
    )(back, table, *parts)


def expert_backward(rows_in, rows_cot, rows_gate, gate_w, up_w, down_w):
    pre_gate = jnp.dot(rows_in, gate_w, preferred_element_type=F32)
    pre_up = jnp.dot(rows_in, up_w, preferred_element_type=F32)
    sigmoid_gate = jax.nn.sigmoid(pre_gate)
    silu_gate = pre_gate * sigmoid_gate
    act = (silu_gate * pre_up).astype(BF)
    expert_out = jnp.dot(act, down_w, preferred_element_type=F32)
    slot_grad = jnp.sum(rows_cot.astype(F32) * expert_out, axis=1).astype(BF)
    d_expert = (rows_gate.astype(F32)[:, None] * rows_cot.astype(F32)).astype(BF)
    d_act = lax.dot_general(d_expert, down_w, (((1,), (1,)), ((), ())), preferred_element_type=F32)
    grad_gate = (d_act * pre_up * sigmoid_gate * (1.0 + pre_gate * (1.0 - sigmoid_gate))).astype(BF)
    grad_up = (d_act * silu_gate).astype(BF)
    across = (((1,), (1,)), ((), ()))
    d_rows = (
        lax.dot_general(grad_gate, gate_w, across, preferred_element_type=F32)
        + lax.dot_general(grad_up, up_w, across, preferred_element_type=F32)
    ).astype(BF)
    return (d_rows, slot_grad, (rows_in, grad_gate, grad_up, act, d_expert))


def body(hidden_in, d_output, gain, route_ids, gates, w_gate, w_up, w_down):
    tok_rows, width = hidden_in.shape
    top_count = route_ids.shape[1]
    seqs = lax.axis_size("seq")
    per_seq = lax.axis_size("expert")
    outer = 4 if per_seq % 4 == 0 else 2
    inner = per_seq // outer
    devices = seqs * per_seq
    experts = w_gate.shape[0] * devices
    capacity = max(2, tok_rows * top_count * 3 // (2 * experts))
    cap = -(-capacity // 8) * 8
    wide_rows = hidden_in.astype(F32)
    inverse_rms = lax.rsqrt(jnp.mean(wide_rows * wide_rows, axis=1, keepdims=True) + 1e-06)
    unit_rows = wide_rows * inverse_rms
    normed = (unit_rows * gain[None, :]).astype(BF)

    ids_t = route_ids.T
    gates_t = gates.T
    names = jnp.arange(experts, dtype=jnp.int32)
    hit = ids_t[:, None, :] == names[None, :, None]
    chosen = jnp.any(hit, axis=0)
    gate_map = jnp.sum(jnp.where(hit, gates_t[:, None, :].astype(F32), 0.0), axis=0)
    token = jnp.arange(tok_rows, dtype=jnp.int32)
    earlier = (token[:, None] < token[None, :]).astype(BF)
    position = jnp.dot(chosen.astype(BF), earlier, preferred_element_type=F32).astype(jnp.int32)
    placed = chosen[:, None, :] & (position[:, None, :] == jnp.arange(cap, dtype=jnp.int32)[None, :, None])
    table = placed.astype(BF)
    gate_table = jnp.where(placed, gate_map[:, None, :], 0.0).astype(BF)
    by_plane = (
        gate_table.reshape(seqs, outer, inner, cap, tok_rows)
        .transpose(1, 0, 2, 3, 4)
        .reshape(outer, seqs * inner * cap, tok_rows)
    )
    got_in, got_cot, tables = dispatch(normed, d_output, by_plane, seqs, outer, inner, cap)
    d_rows, slot_grad, parts = expert_backward(
        got_in.reshape(-1, width), got_cot[:, :, :width].reshape(-1, width),
        got_cot[:, :, width].reshape(-1),
        w_gate[0], w_up[0], w_down[0],
    )
    back = jnp.concatenate(
        [d_rows, jnp.broadcast_to(slot_grad[:, None], (slot_grad.shape[0], LANES))], axis=1
    ).reshape(devices, cap, width + LANES)
    d_normed, grad_map, grad_gate_w, grad_up_w, grad_down_w = collect(
        back, tables, parts, seqs, outer, inner
    )
    lane = jnp.arange(LANES, dtype=jnp.int32)
    ids_column = (
        route_ids // inner % outer * (seqs * inner) + route_ids // per_seq * inner + route_ids % inner
    )
    d_gates = jnp.sum(
        jnp.where(ids_column[:, :, None] == lane[None, None, :], grad_map[:, None, :], 0.0), axis=2
    ).astype(BF)
    gain_term = jnp.sum(d_normed * unit_rows, axis=0)
    gain_parts = lax.all_to_all(
        gain_term.reshape(devices, -1), AXES, split_axis=0, concat_axis=0, tiled=True
    )
    d_gain = jnp.sum(gain_parts, axis=0)
    d_unit = d_normed * gain[None, :]
    inner_mean = jnp.mean(d_unit * unit_rows, axis=1, keepdims=True)
    d_hidden_in = (
        d_output.astype(F32) + inverse_rms * (d_unit - unit_rows * inner_mean)
    ).astype(BF)
    return (d_hidden_in, d_gain, d_gates, grad_gate_w[None], grad_up_w[None], grad_down_w[None])


def solution(mesh):
    rows = P(AXES, None)
    blocks = P(AXES, None, None)
    return jax.shard_map(
        body,
        mesh=mesh,
        in_specs=(rows, rows, P(), rows, rows, blocks, blocks, blocks),
        out_specs=(rows, P(AXES), rows, blocks, blocks, blocks),
        check_vma=False,
    )
```
